256 devices in a mesh: band: 8 (over x, core), grid: 32 (over z, y).
Axes of the slice: x: 4, y: 4, z: 8, core: 2. Of those that a mesh axis runs over, the one named last changes fastest.
Arguments:
- coeffs: float32 [2, 8, 22016, 128], P(None, 'band', 'grid'), may hold values from -6 to 6
- stick_ids: int32 [22016], replicated, may hold values from -1 to 16383, as said below
- band_weights: float32 [8], P('band'), may hold values from 0.02 to 0.2
- aug_functions: float32 [128, 16, 256], replicated, may hold values from -0.1875 to 0.1875
- atom_offsets: int32 [64, 3], replicated, may hold values from 0 to 255, as said below
- intersection_list: int32 [32, 7], P('grid'), may hold values from 0 to 63, as said below
- atom_slots: int32 [128], replicated, may hold values from -1 to 63, as said below
Outputs:
- density: float32 [256, 256, 256], P('grid', 'band')
- atom_totals: float32 [128, 128, 128], P('grid')
The draws below stay inside these ranges and needn't reach their ends.
Inputs may be any that keep to these rules, and one draw needn't show every extreme that they name: `stick_ids`: every column of the 128 x 128 wave-vector columns stands in exactly one slot; empty slots hold -1; some index of grid has all its 688 slots filled. `atom_slots`: every atom stands in exactly one slot; empty slots hold -1; some index of grid has all its 4 slots filled. `atom_offsets`: columns are x0, y0, z0; atom a has z0 in a * 4 .. (a + 1) * 4 - 1. `intersection_list`: row d names 7 distinct atoms, among them every atom whose box has a layer on the planes of index d of grid.
All inputs are finite; a program needn't handle non-finite values.
Results may differ from the reference program's by a relative error of at most 0.0003.
Values sent between devices are 32-bit elements; how exact they have to be, the bound alone decides.
A program may use at most 192 MiB of HBM per device.

```python
import math
import jax
import jax.numpy as jnp
from jax import lax

GRID = 256
KG = 128
PLANES = 8
BOX = 16
NFUNC = 128
NBANDS = 8
N_ATOMS = 64
OWN_CAP = 4
SLOTS = 128
OVL_CAP = 7
STICK_CAP = 688
STICK_SLOTS = 22016
N_GRID = 32


def atom_depths(key):
    spacing = GRID // N_ATOMS
    jitter = jax.random.randint(jax.random.fold_in(key, 11), (N_ATOMS,), 0, spacing, dtype=jnp.int32)
    return (jnp.arange(N_ATOMS, dtype=jnp.int32) * spacing + jitter).astype(jnp.int32)


def draw_atom_offsets(key, part):
    across = jax.random.randint(jax.random.fold_in(key, 12), (N_ATOMS, 2), 0, GRID, dtype=jnp.int32).astype(jnp.int32)
    return jnp.concatenate([across, atom_depths(key)[:, None].astype(jnp.int32)], axis=1).astype(jnp.int32)


def draw_intersection_list(key, part):
    device_count = STICK_SLOTS // STICK_CAP
    planes = GRID // device_count
    first = jnp.arange(device_count, dtype=jnp.int32)[:, None] * planes
    lowest = atom_depths(key)[None, :]
    meets = ((first - lowest) % GRID < BOX) | ((lowest - first) % GRID < planes)
    keys = jax.random.split(jax.random.fold_in(key, 13), device_count)
    ranks = jax.vmap(lambda inner: jax.random.permutation(inner, N_ATOMS).astype(jnp.int32))(keys)
    scores = (jnp.where(meets, 0, N_ATOMS).astype(jnp.int32) + ranks).astype(jnp.int32)
    order = jnp.argsort(scores, axis=1, stable=True)
    return order[:, :OVL_CAP].astype(jnp.int32)


def spread_slots(key, items, capacity, total_slots):
    device_count = total_slots // capacity
    full_row = jax.random.randint(jax.random.fold_in(key, 1), (), 0, device_count, dtype=jnp.int32).astype(jnp.int32)
    item_order = jax.random.permutation(jax.random.fold_in(key, 2), items).astype(jnp.int32)
    others = jax.random.permutation(jax.random.fold_in(key, 3), total_slots - capacity)[:items - capacity].astype(jnp.int32)
    others = (others + capacity * (others // capacity >= full_row).astype(jnp.int32)).astype(jnp.int32)
    owned = (full_row * capacity + jnp.arange(capacity, dtype=jnp.int32)).astype(jnp.int32)
    chosen = jnp.concatenate([owned, others]).astype(jnp.int32)
    return jnp.full((total_slots,), -1, jnp.int32).at[chosen].set(item_order)


def draw_stick_ids(key, part):
    return spread_slots(jax.random.fold_in(key, 21), KG * KG, STICK_CAP, STICK_SLOTS)


def draw_atom_slots(key, part):
    return spread_slots(jax.random.fold_in(key, 31), N_ATOMS, OWN_CAP, SLOTS)


def block_levels(key, shape, cuts, low, high):
    factor_of = 1.0
    for axis_at, parts in cuts:
        draws = jax.random.uniform(jax.random.fold_in(jax.random.fold_in(key, 6), axis_at), (parts,), jnp.float32, low / len(cuts), high / len(cuts))
        factor_of = factor_of * jnp.repeat(jnp.exp(draws), shape[axis_at] // parts).reshape((-1,) + (1,) * (len(shape) - 1 - axis_at))
    return factor_of


def centred(key, shape, deviation, reach, cuts=(), kind=jnp.bfloat16):
    loudness = block_levels(key, shape, cuts, -0.22, 0.18) if cuts else 1.0
    values = jax.random.normal(key, shape, jnp.float32) * deviation * loudness
    return jnp.minimum(jnp.maximum(values, -reach), reach).astype(kind)


def setup_inputs(seed: int = 0) -> dict:
    key_of = jax.random.split(jax.random.key(seed), 8)
    return {
        "coeffs": centred(key_of[0], (2, NBANDS, STICK_SLOTS, KG), 1.0, 6.0, ((1, 8), (2, 32)), jnp.float32),
        "stick_ids": draw_stick_ids(jax.random.fold_in(key_of[7], 71), 0),
        "band_weights": jnp.clip(jnp.exp(math.log(0.2) - 2.3025851 * jax.random.uniform(key_of[2], (NBANDS,), jnp.float32) ** block_levels(key_of[2], (NBANDS,), ((0, 8),), -0.2, 0.2)), 0.02, 0.2),
        "aug_functions": centred(key_of[3], (NFUNC, BOX, BOX * BOX), (BOX * BOX * BOX // 4) ** -0.5, 0.1875, (), jnp.float32),
        "atom_offsets": draw_atom_offsets(jax.random.fold_in(key_of[7], 71), 0),
        "intersection_list": draw_intersection_list(jax.random.fold_in(key_of[7], 71), 0),
        "atom_slots": draw_atom_slots(jax.random.fold_in(key_of[7], 71), 0),
    }


HIGH = lax.Precision.HIGHEST


def column_slots(stick_ids):
    total = KG * KG
    target = jnp.where(stick_ids >= 0, stick_ids, jnp.int32(total)).astype(jnp.int32)
    filled = jnp.zeros((total + 1,), jnp.int32).at[target].set(jnp.arange(stick_ids.shape[0], dtype=jnp.int32))
    return filled[:total]


def layer_pick(first, lowest, layers):
    planes_here = (first + jnp.arange(PLANES, dtype=jnp.int32)).astype(jnp.int32)
    depth = ((planes_here - lowest) % GRID).astype(jnp.int32)
    return (depth[:, None] == layers[None, :]).astype(jnp.float32)


def wrap_pad(field):
    field = jnp.concatenate([field, field[..., :BOX, :]], axis=-2)
    return jnp.concatenate([field, field[..., :BOX]], axis=-1)


def fold_pad(padded):
    rows = padded[:, :GRID, :] + jnp.pad(padded[:, GRID:, :], ((0, 0), (0, GRID - BOX), (0, 0)))
    return rows[:, :, :GRID] + jnp.pad(rows[:, :, GRID:], ((0, 0), (0, 0), (0, GRID - BOX)))


def wave_of(band_coeffs, slot_map):
    spectra = band_coeffs[:, slot_map, :].reshape(2, KG, KG, KG)
    places = ((jnp.arange(KG, dtype=jnp.int32) - KG // 2) % GRID).astype(jnp.int32)
    empty = jnp.zeros((GRID, GRID, GRID), jnp.float32)
    real_full = empty.at[places[:, None, None], places[None, :, None], places[None, None, :]].set(spectra[0])
    imag_full = empty.at[places[:, None, None], places[None, :, None], places[None, None, :]].set(spectra[1])
    field = jnp.fft.ifftn(lax.complex(real_full, imag_full)) * (float(GRID) ** 3 * float(KG) ** -1.5)
    return jnp.transpose(jnp.real(field), (2, 0, 1)), jnp.transpose(jnp.imag(field), (2, 0, 1))


def reference(coeffs, stick_ids, band_weights, aug_functions, atom_offsets, intersection_list, atom_slots):
    slot_map = column_slots(stick_ids)
    every_layer = jnp.arange(BOX, dtype=jnp.int32)
    device_rows = jnp.arange(N_GRID, dtype=jnp.int32)

    def band_step(carry, inputs):
        density, matrices = carry
        band_coeffs, weight = inputs
        real_wave, imag_wave = wave_of(band_coeffs, slot_map)
        density = density + weight * (real_wave * real_wave + imag_wave * imag_wave)
        wave = jnp.stack([real_wave, imag_wave])

        def device_step(found, row):
            first = (row * PLANES).astype(jnp.int32)
            padded = wrap_pad(lax.dynamic_slice_in_dim(wave, first, PLANES, 1))

            def one_atom(atom):
                offsets = atom_offsets[atom].astype(jnp.int32)
                pick = layer_pick(first, offsets[2], every_layer)
                chosen = jnp.einsum("pk,ikc->ipc", pick, aug_functions, precision=HIGH)
                window = lax.dynamic_slice(padded, (jnp.int32(0), jnp.int32(0), offsets[0], offsets[1]), (2, PLANES, BOX, BOX))
                window = window.reshape(2, PLANES, BOX * BOX)
                return jnp.einsum("ipc,xpc->xi", chosen, window, precision=HIGH)

            listed = intersection_list[row].astype(jnp.int32)
            return found.at[listed].add(jax.vmap(one_atom)(listed)), None

        found, _ = lax.scan(device_step, jnp.zeros((N_ATOMS, 2, NFUNC), jnp.float32), device_rows)
        matrices = matrices + weight * jnp.einsum("axi,axj->aij", found, found, precision=HIGH)
        return (density, matrices), None

    start = (jnp.zeros((GRID, GRID, GRID), jnp.float32), jnp.zeros((N_ATOMS, NFUNC, NFUNC), jnp.float32))
    (density, matrices), _ = lax.scan(band_step, start, (jnp.moveaxis(coeffs, 1, 0), band_weights))

    safe_slots = jnp.maximum(atom_slots, 0).astype(jnp.int32)
    atom_totals = jnp.where((atom_slots >= 0)[:, None, None], matrices[safe_slots], 0.0)

    flat = aug_functions.reshape(NFUNC, BOX * BOX * BOX)

    def expand(matrix):
        return jnp.sum(flat * jnp.dot(matrix, flat, precision=HIGH), axis=0).reshape(BOX, BOX * BOX)

    boxes = lax.map(expand, matrices)

    def add_step(dummy, row):
        first = (row * PLANES).astype(jnp.int32)
        listed = intersection_list[row].astype(jnp.int32)

        def one_atom(atom):
            offsets = atom_offsets[atom].astype(jnp.int32)
            pick = layer_pick(first, offsets[2], every_layer)
            return jnp.dot(pick, boxes[atom], precision=HIGH).reshape(PLANES, BOX, BOX)

        pieces = jax.vmap(one_atom)(listed)
        listed_offsets = atom_offsets[listed].astype(jnp.int32)

        def place(index, acc):
            corner = (jnp.int32(0), listed_offsets[index, 0], listed_offsets[index, 1])
            current = lax.dynamic_slice(acc, corner, (PLANES, BOX, BOX))
            return lax.dynamic_update_slice(acc, current + pieces[index], corner)

        part = lax.fori_loop(0, OVL_CAP, place, jnp.zeros((PLANES, GRID + BOX, GRID + BOX), jnp.float32))
        return dummy, fold_pad(part)

    _, extra = lax.scan(add_step, jnp.zeros((), jnp.float32), device_rows)
    density = density + extra.reshape(GRID, GRID, GRID)
    return density, atom_totals
```

```python
import functools

import jax
import jax.numpy as jnp
import numpy as np
from jax import lax
from jax.experimental import pallas as pl
from jax.experimental.pallas import tpu as pltpu
from jax.sharding import PartitionSpec as P

GRID = 256
KG = 128
PLANES = 8
BOX = 16
NFUNC = 128
NBANDS = 8
N_GRID = 32
N_ATOMS = 64
OWN = 4
CAP = 688
NEAR = 6
BF = jnp.bfloat16
F32 = jnp.float32
VM = pl.BlockSpec(memory_space=pltpu.VMEM)
SM = pl.BlockSpec(memory_space=pltpu.SMEM)
ANY = pl.BlockSpec(memory_space=pl.ANY)
NT = (((1,), (1,)), ((), ()))
NN = (((1,), (0,)), ((), ()))


def tables():
    frequency = np.arange(KG) - KG // 2
    angles = 2.0 * np.pi * ((frequency[:, None] * np.arange(GRID)[None, :]) % GRID) / GRID
    cosine = np.cos(angles) * KG ** -0.5
    sine = np.sin(angles) * KG ** -0.5
    to_real = np.concatenate([cosine, -sine], axis=0)
    to_imag = np.concatenate([sine, cosine], axis=0)
    along_z = np.stack([to_real.T, to_imag.T]).reshape(2, N_GRID, PLANES, 2 * KG)
    along_z = along_z.transpose(1, 0, 2, 3).reshape(2 * GRID, 2 * KG)
    along_y = np.concatenate([to_real, to_imag], axis=1)
    along_x = np.concatenate([to_real.T, to_imag.T], axis=0)
    return along_z, along_y, along_x


def halves(table):
    high = table.astype(np.float32).astype(BF)
    low = (table - high.astype(np.float64)).astype(np.float32).astype(BF)
    return high, low


def split(value):
    high = value.astype(BF)
    return high, (value - high.astype(F32)).astype(BF)


def mm(left, right, dims=NN):
    return lax.dot_general(left, right, dims, preferred_element_type=F32)


def mm3(left, right, dims=NN):
    return mm(left[0], right[0], dims) + mm(left[1], right[0], dims) + mm(left[0], right[1], dims)


def z_kernel(c_ref, high_ref, low_ref, out_ref):
    both = jnp.concatenate([c_ref[0], c_ref[1]], axis=1)
    parts = split(both)
    for chunk in range(4):
        rows = pl.ds(chunk * 128, 128)
        got = mm3((high_ref[rows, :], low_ref[rows, :]), parts, NT)
        out_ref[pl.ds(chunk * 8, 8)] = got.reshape(8, 16, CAP)


def z_transform(coeffs, high, low):
    return pl.pallas_call(
        z_kernel,
        out_shape=jax.ShapeDtypeStruct((N_GRID, 16, CAP), F32),
        in_specs=[VM] * 3,
        out_specs=VM,
        name="z_transform",
    )(coeffs, high, low)


def exchange_kernel(in_ref, out_ref, own, local_sem, send_sem, recv_sem):
    me = lax.axis_index("grid")
    barrier = pltpu.get_barrier_semaphore()

    def peer(step):
        dz, dy = step // 4, step % 4
        return ((me // 4 + dz) % 8) * 4 + (me % 4 + dy) % 4

    for step in range(1, N_GRID):
        pl.semaphore_signal(barrier, inc=1, device_id={"grid": peer(step)})
    pl.semaphore_wait(barrier, N_GRID - 1)
    copies = []
    for step in ORDER:
        target = peer(step)
        copy = pltpu.make_async_remote_copy(
            src_ref=in_ref.at[target],
            dst_ref=out_ref.at[me],
            send_sem=send_sem.at[step],
            recv_sem=recv_sem.at[step],
            device_id={"grid": target},
        )
        copy.start()
        copies.append(copy)
    first = pltpu.make_async_copy(in_ref.at[me], own, local_sem)
    first.start()
    first.wait()
    second = pltpu.make_async_copy(own, out_ref.at[me], local_sem)
    second.start()
    second.wait()
    for copy in copies:
        copy.wait()


ORDER = sorted(range(1, N_GRID), key=lambda step: (-min(step // 4, 8 - step // 4), step % 4, step))


def exchange(sticks):
    return pl.pallas_call(
        exchange_kernel,
        out_shape=jax.ShapeDtypeStruct((N_GRID, 16, CAP), F32),
        in_specs=[ANY],
        out_specs=ANY,
        scratch_shapes=[
            pltpu.VMEM((16, CAP), F32),
            pltpu.SemaphoreType.DMA,
            pltpu.SemaphoreType.DMA((N_GRID,)),
            pltpu.SemaphoreType.DMA((N_GRID,)),
        ],
        compiler_params=pltpu.CompilerParams(collective_id=0, has_side_effects=True),
        name="stick_exchange",
    )(sticks)


def window_pick(y0):
    cell = lax.broadcasted_iota(jnp.int32, (GRID, GRID), 1)
    place = lax.broadcasted_iota(jnp.int32, (GRID, GRID), 0)
    return (place == (y0 + cell % BOX) % GRID).astype(F32).astype(BF)


def wave_kernel(ids, offsets, weight, sticks, yh, yl, xh, xl, aug, dens, proj, stage, cols, lhs_h, lhs_l, spec, wave, rows):
    me = lax.axis_index("grid")

    def one_source(source, carry):
        for first in range(0, CAP, 128):
            size = min(128, CAP - first)
            block = sticks[source, :, pl.ds(first, size)]
            wide = jnp.broadcast_to(block[:, None, :], (16, 8, size)).reshape(128, size)
            stage[pl.ds(first, size), :] = jnp.transpose(wide)
        base = source * CAP
        for first in range(0, CAP, 16):
            held = [stage[pl.ds(first + j, 1), :] for j in range(16)]
            for j in range(16):
                cols[pl.ds(ids[base + first + j] + 8, 1), :] = held[j]
        return carry

    lax.fori_loop(0, N_GRID, one_source, 0)

    lane = lax.broadcasted_iota(jnp.int32, (128, 128), 1) % 8

    def pack(block, carry):
        packed = cols[pl.ds(pl.multiple_of(block * 1024 + 8, 8), 128), :]
        for k in range(1, 8):
            here = cols[pl.ds(pl.multiple_of(block * 1024 + 8 + k * 128, 8), 128), :]
            packed = jnp.where(lane == k, here, packed)
        turned = jnp.transpose(packed)
        both = jnp.concatenate([turned[:64], turned[64:]], axis=1)
        high, low = split(both)
        where = pl.ds(pl.multiple_of(block * 64, 64), 64)
        lhs_h[where, :] = high
        lhs_l[where, :] = low
        return carry

    lax.fori_loop(0, 16, pack, 0)

    def y_step(chunk, carry):
        where = pl.ds(pl.multiple_of(chunk * 256, 256), 256)
        got = mm3((lhs_h[where, :], lhs_l[where, :]), (yh[...], yl[...]))
        got = got.reshape(4, 8, 8, 512)
        for part in range(4):
            first = pl.multiple_of(chunk * 32 + part * 8, 8)
            spec[:, pl.ds(first, 8), :] = got[part, :, :, :GRID]
            spec[:, pl.ds(first + KG, 8), :] = got[part, :, :, GRID:]
        return carry

    lax.fori_loop(0, 4, y_step, 0)

    scale = weight[0]

    def x_step(plane, carry):
        got = mm3((xh[...], xl[...]), split(spec[plane]))
        real, imag = got[:GRID], got[GRID:]
        wave[plane, 0, pl.ds(0, GRID), :] = real
        wave[plane, 1, pl.ds(0, GRID), :] = imag
        wave[plane, 0, pl.ds(GRID, 24), :] = real[:24]
        wave[plane, 1, pl.ds(GRID, 24), :] = imag[:24]
        dens[plane] = scale * (real * real + imag * imag)
        return carry

    lax.fori_loop(0, PLANES, x_step, 0)

    rows[...] = jnp.zeros_like(rows)
    cell = lax.broadcasted_iota(jnp.int32, (24, GRID), 1) // BOX
    row = lax.broadcasted_iota(jnp.int32, (24, GRID), 0)

    def one_atom(m, carry):
        atom = (2 * me - 4 + m + N_ATOMS) % N_ATOMS
        x0, y0, z0 = offsets[3 * atom], offsets[3 * atom + 1], offsets[3 * atom + 2]
        low_x = pl.multiple_of((x0 // 8) * 8, 8)
        window = wave[:, :, pl.ds(low_x, 24), :].reshape(16 * 24, GRID)
        high, low = split(window)
        pick = window_pick(y0)
        picked = (mm(high, pick) + mm(low, pick)).reshape(16, 24, GRID)
        keep = cell == row - (x0 - low_x)
        flat = jnp.sum(jnp.where(keep[None], picked, 0.0), axis=1)
        flat = flat.reshape(8, 2, GRID)
        for plane in range(PLANES):
            k = (me * PLANES + plane - z0 + GRID) % GRID

            @pl.when(k < BOX)
            def _():
                rows[k, pl.ds(2 * m, 2), :] = flat[plane]

        return carry

    for m in range(NEAR):
        one_atom(m, 0)

    def contract(k, total):
        return total + mm3(split(rows[k]), split(aug[k]), NT)

    proj[...] = lax.fori_loop(0, BOX, contract, jnp.zeros((16, NFUNC), F32))


def waves(ids, offsets, weight, sticks, yh, yl, xh, xl, aug):
    return pl.pallas_call(
        wave_kernel,
        out_shape=(
            jax.ShapeDtypeStruct((PLANES, GRID, GRID), F32),
            jax.ShapeDtypeStruct((16, NFUNC), F32),
        ),
        in_specs=[SM, SM, SM] + [VM] * 6,
        out_specs=(VM, VM),
        scratch_shapes=[
            pltpu.VMEM((CAP, 128), F32),
            pltpu.VMEM((KG * KG + 8, 128), F32),
            pltpu.VMEM((1024, GRID), BF),
            pltpu.VMEM((1024, GRID), BF),
            pltpu.VMEM((PLANES, GRID, GRID), F32),
            pltpu.VMEM((PLANES, 2, GRID + 24, GRID), F32),
            pltpu.VMEM((BOX, 16, GRID), F32),
        ],
        name="waves",
    )(ids, offsets, weight, sticks, yh, yl, xh, xl, aug)


def spread_kernel(proj, dens, every, slabs, own, local_sem, proj_send, proj_recv, dens_send, dens_recv):
    me = lax.axis_index("grid")
    band = lax.axis_index("band")
    barrier = pltpu.get_barrier_semaphore()
    for step in range(1, N_GRID):
        pl.semaphore_signal(barrier, inc=1, device_id={"grid": (me + step) % N_GRID})
    for step in range(1, NBANDS):
        pl.semaphore_signal(barrier, inc=1, device_id={"band": (band + step) % NBANDS})
    pl.semaphore_wait(barrier, N_GRID + NBANDS - 2)
    copies = []
    for step in range(1, N_GRID):
        target = (me + step) % N_GRID
        copies.append(
            pltpu.make_async_remote_copy(
                src_ref=proj,
                dst_ref=every.at[me],
                send_sem=proj_send.at[step],
                recv_sem=proj_recv.at[step],
                device_id={"grid": target},
            )
        )
    for step in range(1, NBANDS):
        target = (band + step) % NBANDS
        copies.append(
            pltpu.make_async_remote_copy(
                src_ref=dens.at[:, pl.ds(pl.multiple_of(target * 32, 32), 32), :],
                dst_ref=slabs.at[band],
                send_sem=dens_send.at[step],
                recv_sem=dens_recv.at[step],
                device_id={"band": target},
            )
        )
    for copy in copies:
        copy.start()
    every[me] = proj[...]
    first = pltpu.make_async_copy(dens.at[:, pl.ds(pl.multiple_of(band * 32, 32), 32), :], own, local_sem)
    first.start()
    first.wait()
    second = pltpu.make_async_copy(own, slabs.at[band], local_sem)
    second.start()
    second.wait()
    for copy in copies:
        copy.wait()


def spread(proj, dens):
    return pl.pallas_call(
        spread_kernel,
        out_shape=(
            jax.ShapeDtypeStruct((N_GRID, 16, NFUNC), F32),
            jax.ShapeDtypeStruct((NBANDS, PLANES, 32, GRID), F32),
        ),
        in_specs=[VM, ANY],
        out_specs=(VM, ANY),
        scratch_shapes=[
            pltpu.VMEM((PLANES, 32, GRID), F32),
            pltpu.SemaphoreType.DMA,
            pltpu.SemaphoreType.DMA((N_GRID,)),
            pltpu.SemaphoreType.DMA((N_GRID,)),
            pltpu.SemaphoreType.DMA((NBANDS,)),
            pltpu.SemaphoreType.DMA((NBANDS,)),
        ],
        compiler_params=pltpu.CompilerParams(collective_id=1, has_side_effects=True),
        name="spread",
    )(proj, dens)


def choose_kernel(slots, weight, every, out):
    me = lax.axis_index("grid")

    def gathered(atom):
        parity = atom % 2
        total = jnp.zeros((2, NFUNC), F32)
        for j in range(3):
            total = total + every[(atom // 2 + j) % N_GRID, pl.ds(2 * (4 - 2 * j) + 2 * parity, 2), :]
        return total

    for m in range(NEAR):
        out[pl.ds(2 * m, 2), :] = gathered((2 * me - 4 + m + N_ATOMS) % N_ATOMS)
    for s in range(OWN):
        atom = slots[me * OWN + s]
        found = gathered(jnp.maximum(atom, 0))
        out[pl.ds(12 + 2 * s, 2), :] = jnp.where(atom >= 0, found, 0.0)
    out[pl.ds(20, 4), :] = jnp.full((4, NFUNC), weight[0], F32)


def choose(slots, weight, every):
    return pl.pallas_call(
        choose_kernel,
        out_shape=jax.ShapeDtypeStruct((24, NFUNC), F32),
        in_specs=[SM, SM, VM],
        out_specs=VM,
        name="choose",
    )(slots, weight, every)


def share_kernel(mine, out, send_sem, recv_sem):
    band = lax.axis_index("band")
    barrier = pltpu.get_barrier_semaphore()
    for step in range(1, NBANDS):
        pl.semaphore_signal(barrier, inc=1, device_id={"band": (band + step) % NBANDS})
    pl.semaphore_wait(barrier, NBANDS - 1)
    copies = []
    for step in range(1, NBANDS):
        target = (band + step) % NBANDS
        copy = pltpu.make_async_remote_copy(
            src_ref=mine,
            dst_ref=out.at[band],
            send_sem=send_sem.at[step],
            recv_sem=recv_sem.at[step],
            device_id={"band": target},
        )
        copy.start()
        copies.append(copy)
    out[band] = mine[...]
    for copy in copies:
        copy.wait()


def share(mine):
    return pl.pallas_call(
        share_kernel,
        out_shape=jax.ShapeDtypeStruct((NBANDS, 24, NFUNC), F32),
        in_specs=[VM],
        out_specs=VM,
        scratch_shapes=[pltpu.SemaphoreType.DMA((NBANDS,)), pltpu.SemaphoreType.DMA((NBANDS,))],
        compiler_params=pltpu.CompilerParams(collective_id=2, has_side_effects=True),
        name="share",
    )(mine)


def final_kernel(offsets, shared, slabs, aug, dens, totals, near, level, boxes):
    me = lax.axis_index("grid")
    band = lax.axis_index("band")
    for m in range(NEAR):
        for b in range(NBANDS):
            near[pl.ds(m * 16 + 2 * b, 2), :] = shared[b, pl.ds(2 * m, 2), :]
    for b in range(NBANDS):
        level[pl.ds(2 * b, 2), :] = shared[b, pl.ds(20, 2), :]
    weights = level[...]
    for s in range(OWN):
        own = jnp.concatenate([shared[b, pl.ds(12 + 2 * s, 2), :] for b in range(NBANDS)], axis=0)
        totals[s] = lax.dot_general(
            own * weights,
            own,
            (((0,), (0,)), ((), ())),
            precision=lax.Precision.HIGHEST,
            preferred_element_type=F32,
        )
    parts = split(near[...])
    wide = jnp.concatenate([weights, weights], axis=1)

    def one_layer(k, carry):
        value = mm3(parts, split(aug[k])).reshape(NEAR, 16, GRID)
        boxes[k, pl.ds(0, NEAR), :] = jnp.sum(value * value * wide[None], axis=1)
        return carry

    lax.fori_loop(0, BOX, one_layer, 0)
    total = slabs[0]
    for b in range(1, NBANDS):
        total = total + slabs[b]
    dens[...] = total
    row = lax.broadcasted_iota(jnp.int32, (32, GRID), 0)
    cell = lax.broadcasted_iota(jnp.int32, (32, GRID), 1) // BOX
    for m in range(NEAR):
        atom = (2 * me - 4 + m + N_ATOMS) % N_ATOMS
        x0, y0, z0 = offsets[3 * atom], offsets[3 * atom + 1], offsets[3 * atom + 2]
        shift = (band * 32 - x0 + GRID) % GRID

        @pl.when((shift < BOX) | (shift > GRID - 32))
        def _():
            keep = cell == (row + shift) % GRID
            planes = []
            for plane in range(PLANES):
                k = (me * PLANES + plane - z0 + GRID) % GRID
                line = boxes[jnp.minimum(k, BOX - 1), pl.ds(m, 1), :]
                line = jnp.where(k < BOX, line, 0.0)
                planes.append(jnp.where(keep, line, 0.0))
            high, low = split(jnp.concatenate(planes, axis=0))
            pick = window_pick(y0)
            spot = mm(high, pick, NT) + mm(low, pick, NT)
            dens[...] += spot.reshape(PLANES, 32, GRID)


def final(offsets, shared, slabs, aug):
    return pl.pallas_call(
        final_kernel,
        out_shape=(
            jax.ShapeDtypeStruct((PLANES, 32, GRID), F32),
            jax.ShapeDtypeStruct((OWN, NFUNC, NFUNC), F32),
        ),
        in_specs=[SM, VM, VM, VM],
        out_specs=(VM, VM),
        scratch_shapes=[
            pltpu.VMEM((NEAR * 16, NFUNC), F32),
            pltpu.VMEM((16, NFUNC), F32),
            pltpu.VMEM((BOX, 8, GRID), F32),
        ],
        name="final",
    )(offsets, shared, slabs, aug)


def on_device(coeffs, stick_ids, band_weights, aug_functions, atom_offsets, intersection_list, atom_slots):
    along_z, along_y, along_x = (halves(table) for table in tables())
    offsets = atom_offsets.reshape(-1)
    aug = jnp.transpose(aug_functions, (1, 0, 2))
    sticks = z_transform(coeffs.reshape(2, CAP, KG), *along_z)
    received = exchange(sticks)
    dens, proj = waves(stick_ids, offsets, band_weights, received, *along_y, *along_x, aug)
    every, slabs = spread(proj, dens)
    shared = share(choose(atom_slots, band_weights, every))
    return final(offsets, shared, slabs, aug)


def solution(mesh):
    placed = (P(None, "band", "grid", None), P(), P("band"), P(), P(), P("grid", None), P())
    return jax.shard_map(
        on_device,
        mesh=mesh,
        in_specs=placed,
        out_specs=(P("grid", "band", None), P("grid", None, None)),
        check_vma=False,
    )
```

```python
import functools

import jax
import jax.numpy as jnp
import numpy as np
from jax import lax
from jax.experimental import pallas as pl
from jax.experimental.pallas import tpu as pltpu
from jax.sharding import PartitionSpec as P

GRID = 256
KG = 128
PLANES = 8
BOX = 16
NFUNC = 128
NBANDS = 8
N_GRID = 32
N_ATOMS = 64
OWN = 4
CAP = 688
NEAR = 6
HIGH = 64
FULL = CAP // 128
REST = CAP % 128
TILES = 2 * FULL + 1
BF = jnp.bfloat16
F32 = jnp.float32
VM = pl.BlockSpec(memory_space=pltpu.VMEM)
SM = pl.BlockSpec(memory_space=pltpu.SMEM)
ANY = pl.BlockSpec(memory_space=pl.ANY)
NT = (((1,), (1,)), ((), ()))
NN = (((1,), (0,)), ((), ()))


def tables():
    frequency = np.arange(KG) - KG // 2
    angles = 2.0 * np.pi * ((frequency[:, None] * np.arange(GRID)[None, :]) % GRID) / GRID
    cosine = np.cos(angles) * KG ** -0.5
    sine = np.sin(angles) * KG ** -0.5
    to_real = np.concatenate([cosine, -sine], axis=0)
    to_imag = np.concatenate([sine, cosine], axis=0)
    along_z = np.stack([to_real.T, to_imag.T]).reshape(2, N_GRID, PLANES, 2 * KG)
    along_z = along_z.transpose(1, 0, 2, 3).reshape(2 * GRID, 2 * KG)
    along_y = np.concatenate([to_real, to_imag], axis=1)
    order = np.concatenate([np.arange(0, KG, 2), np.arange(1, KG, 2)])
    order = np.concatenate([order, order + KG])
    along_x = np.concatenate([to_real.T, to_imag.T], axis=0)[:, order]
    return along_z, along_y, along_x


def halves(table):
    high = table.astype(np.float32).astype(BF)
    low = (table - high.astype(np.float64)).astype(np.float32).astype(BF)
    return high, low


def split(value):
    high = value.astype(BF)
    return high, (value - high.astype(F32)).astype(BF)


def mm(left, right, dims=NN):
    return lax.dot_general(left, right, dims, preferred_element_type=F32)


def mm3(left, right, dims=NN):
    return mm(left[0], right[0], dims) + mm(left[1], right[0], dims) + mm(left[0], right[1], dims)


def z_kernel(c_ref, high_ref, low_ref, out_ref):
    both = jnp.concatenate([c_ref[0], c_ref[1]], axis=1)
    parts = split(both)
    for chunk in range(4):
        rows = pl.ds(chunk * 128, 128)
        got = mm3((high_ref[rows, :], low_ref[rows, :]), parts, NT).reshape(8, 16, CAP)
        where = pl.ds(chunk * 8, 8)
        for tile in range(FULL):
            lanes = slice(tile * 128, tile * 128 + 128)
            out_ref[where, 2 * tile] = got[:, :8, lanes]
            out_ref[where, 2 * tile + 1] = got[:, 8:, lanes]
        rest = got[:, :, FULL * 128 :]
        blank = jnp.zeros((8, 8, 128 - 2 * REST), F32)
        out_ref[where, 2 * FULL] = jnp.concatenate([rest[:, :8], rest[:, 8:], blank], axis=2)


def z_transform(coeffs, high, low):
    return pl.pallas_call(
        z_kernel,
        out_shape=jax.ShapeDtypeStruct((N_GRID, TILES, 8, 128), F32),
        in_specs=[VM] * 3,
        out_specs=VM,
        name="z_transform",
    )(coeffs, high, low)


def exchange_kernel(ids, in_ref, aug, grid, aug_h, aug_l, land, held, local_sem, aug_sem, send_sem, recv_sem):
    me = lax.axis_index("grid")
    z, y = me // 4, me % 4
    barrier = pltpu.get_barrier_semaphore()

    def offset(step):
        turn = (step + 28) % N_GRID
        part = turn // 4
        return 4 + ((part + 1) // 2) * (1 - 2 * (part % 2)), turn % 4

    def copy_at(step):
        dz, dy = offset(step)
        target = ((z + dz) % 8) * 4 + (y + dy) % 4
        return pltpu.make_async_remote_copy(
            src_ref=in_ref.at[target],
            dst_ref=land.at[me],
            send_sem=send_sem.at[step],
            recv_sem=recv_sem.at[step],
            device_id={"grid": target},
        )

    for step in range(1, N_GRID):
        pl.semaphore_signal(barrier, inc=1, device_id={"grid": (me + step) % N_GRID})
    pl.semaphore_wait(barrier, N_GRID - 1)
    for step in range(1, N_GRID):
        copy_at(step).start()
    mine = pltpu.make_async_copy(in_ref.at[me], land.at[me], local_sem)
    mine.start()
    fetch = pltpu.make_async_copy(aug, held, aug_sem)
    fetch.start()
    grid[...] = jnp.zeros_like(grid)
    mine.wait()
    fetch.wait()
    for k in range(BOX):
        high, low = split(held[:, k, :])
        aug_h[k] = high
        aug_l[k] = low

    row = lax.broadcasted_iota(jnp.int32, (HIGH, CAP), 0)
    column = lax.broadcasted_iota(jnp.int32, (GRID, CAP), 0)

    def one_source(step, carry):
        @pl.when(step > 0)
        def _():
            copy_at(step).wait()

        dz, dy = offset(step)
        source = ((z - dz + 8) % 8) * 4 + (y - dy + 4) % 4
        name = ids[source]
        in_row = (row == (name >> 8)).astype(F32).astype(BF)
        in_column = (column == (name & (GRID - 1))).astype(F32).astype(BF)
        tiles = land[source]
        top = [tiles[2 * tile] for tile in range(FULL)] + [tiles[2 * FULL][:, :REST]]
        bottom = [tiles[2 * tile + 1] for tile in range(FULL)] + [tiles[2 * FULL][:, REST : 2 * REST]]
        value = jnp.concatenate([jnp.concatenate(top, axis=1), jnp.concatenate(bottom, axis=1)], axis=0)
        both = jnp.concatenate(split(value), axis=0)
        left = (in_row[None] * both[:, None, :]).reshape(32 * HIGH, CAP)
        got = mm(left, in_column, NT)
        grid[...] += (got[: 16 * HIGH] + got[16 * HIGH :]).reshape(16, HIGH, GRID)
        return carry

    lax.fori_loop(0, N_GRID, one_source, 0)


def exchange(ids, sticks, aug):
    return pl.pallas_call(
        exchange_kernel,
        out_shape=(
            jax.ShapeDtypeStruct((16, HIGH, GRID), F32),
            jax.ShapeDtypeStruct((BOX, NFUNC, GRID), BF),
            jax.ShapeDtypeStruct((BOX, NFUNC, GRID), BF),
        ),
        in_specs=[VM, ANY, ANY],
        out_specs=(VM, VM, VM),
        scratch_shapes=[
            pltpu.VMEM((N_GRID, TILES, 8, 128), F32),
            pltpu.VMEM((NFUNC, BOX, GRID), F32),
            pltpu.SemaphoreType.DMA,
            pltpu.SemaphoreType.DMA,
            pltpu.SemaphoreType.DMA((N_GRID,)),
            pltpu.SemaphoreType.DMA((N_GRID,)),
        ],
        compiler_params=pltpu.CompilerParams(collective_id=0, has_side_effects=True),
        name="stick_exchange",
    )(ids, sticks, aug)


def window_pick(y0):
    cell = lax.broadcasted_iota(jnp.int32, (GRID, GRID), 1)
    place = lax.broadcasted_iota(jnp.int32, (GRID, GRID), 0)
    return (place == (y0 + cell % BOX) % GRID).astype(F32).astype(BF)


def wave_kernel(offsets, weight, grid, yh, yl, xh, xl, aug_h, aug_l, dens, proj, spec, wave, rows):
    me = lax.axis_index("grid")
    for parity in range(2):
        lanes = slice(parity * KG, parity * KG + KG)
        both = jnp.concatenate([grid[:8, :, lanes], grid[8:, :, lanes]], axis=2).reshape(8 * HIGH, GRID)
        got = mm3(split(both), (yh[...], yl[...])).reshape(8, HIGH, 2 * GRID)
        spec[:, pl.ds(parity * HIGH, HIGH), :] = got[:, :, :GRID]
        spec[:, pl.ds(parity * HIGH + KG, HIGH), :] = got[:, :, GRID:]

    scale = weight[0]

    def x_step(plane, carry):
        got = mm3((xh[...], xl[...]), split(spec[plane]))
        real, imag = got[:GRID], got[GRID:]
        wave[plane, 0, pl.ds(0, GRID), :] = real
        wave[plane, 1, pl.ds(0, GRID), :] = imag
        wave[plane, 0, pl.ds(GRID, 24), :] = real[:24]
        wave[plane, 1, pl.ds(GRID, 24), :] = imag[:24]
        local = (scale * (real * real + imag * imag)).reshape(4, 2, 32, GRID)
        dens[0, :, plane] = local[:, 0]
        dens[1, :, plane] = local[:, 1]
        return carry

    lax.fori_loop(0, PLANES, x_step, 0)

    rows[...] = jnp.zeros_like(rows)
    cell = lax.broadcasted_iota(jnp.int32, (24, GRID), 1) // BOX
    row = lax.broadcasted_iota(jnp.int32, (24, GRID), 0)

    def one_atom(m, carry):
        atom = (2 * me - 4 + m + N_ATOMS) % N_ATOMS
        x0, y0, z0 = offsets[0, atom], offsets[1, atom], offsets[2, atom]
        low_x = pl.multiple_of((x0 // 8) * 8, 8)
        window = wave[:, :, pl.ds(low_x, 24), :].reshape(16 * 24, GRID)
        high, low = split(window)
        pick = window_pick(y0)
        picked = (mm(high, pick) + mm(low, pick)).reshape(16, 24, GRID)
        keep = cell == row - (x0 - low_x)
        flat = jnp.sum(jnp.where(keep[None], picked, 0.0), axis=1)
        flat = flat.reshape(8, 2, GRID)
        for plane in range(PLANES):
            k = (me * PLANES + plane - z0 + GRID) % GRID

            @pl.when(k < BOX)
            def _():
                rows[k, pl.ds(2 * m, 2), :] = flat[plane]

        return carry

    for m in range(NEAR):
        one_atom(m, 0)

    def contract(k, total):
        return total + mm3(split(rows[k]), (aug_h[k], aug_l[k]), NT)

    proj[...] = lax.fori_loop(0, BOX, contract, jnp.zeros((16, NFUNC), F32))


def waves(offsets, weight, grid, yh, yl, xh, xl, aug_h, aug_l):
    return pl.pallas_call(
        wave_kernel,
        out_shape=(
            jax.ShapeDtypeStruct((2, 4, PLANES, 32, GRID), F32),
            jax.ShapeDtypeStruct((16, NFUNC), F32),
        ),
        in_specs=[SM, SM] + [VM] * 7,
        out_specs=(VM, VM),
        scratch_shapes=[
            pltpu.VMEM((PLANES, GRID, GRID), F32),
            pltpu.VMEM((PLANES, 2, GRID + 24, GRID), F32),
            pltpu.VMEM((BOX, 16, GRID), F32),
        ],
        name="waves",
    )(offsets, weight, grid, yh, yl, xh, xl, aug_h, aug_l)


def sum_kernel(
    slots, weight, proj, dens, aug_h, aug_l, total, shared, boxes,
    every, mine, near, level, half, other, summed, slabs,
    half_sem, pair_send, pair_recv, slab_send, slab_recv, proj_send, proj_recv, share_send, share_recv,
):
    me = lax.axis_index("grid")
    band = lax.axis_index("band")
    chip, core = band // 2, band % 2
    partner = chip * 2 + 1 - core
    barrier = pltpu.get_barrier_semaphore()
    for step in range(1, N_GRID):
        pl.semaphore_signal(barrier, inc=1, device_id={"grid": (me + step) % N_GRID})
    for step in range(1, NBANDS):
        pl.semaphore_signal(barrier, inc=1, device_id={"band": (band + step) % NBANDS})
    fetches = []
    for step in range(4):
        place = (chip + step) % 4
        fetches.append(pltpu.make_async_copy(dens.at[core, place], half.at[step], half_sem.at[step]))
        fetches[-1].start()
    pl.semaphore_wait(barrier, N_GRID + NBANDS - 2)

    pairs, slab_copies = [], []
    for step in range(4):
        place = (chip + step) % 4
        pairs.append(
            pltpu.make_async_remote_copy(
                src_ref=dens.at[1 - core, place],
                dst_ref=other.at[step],
                send_sem=pair_send.at[step],
                recv_sem=pair_recv.at[step],
                device_id={"band": partner},
            )
        )
        slab_copies.append(
            None
            if step == 0
            else pltpu.make_async_remote_copy(
                src_ref=summed.at[step],
                dst_ref=slabs.at[step],
                send_sem=slab_send.at[step],
                recv_sem=slab_recv.at[step],
                device_id={"band": place * 2 + core},
            )
        )
    pairs[2].start()
    proj_copies = []
    for step in range(1, N_GRID):
        copy = pltpu.make_async_remote_copy(
            src_ref=proj,
            dst_ref=every.at[me],
            send_sem=proj_send.at[step],
            recv_sem=proj_recv.at[step],
            device_id={"grid": (me + step) % N_GRID},
        )
        copy.start()
        proj_copies.append(copy)
    for step in (1, 3, 0):
        pairs[step].start()
    every[me] = proj[...]

    def combine(step):
        fetches[step].wait()
        pairs[step].wait()
        summed[step] = half[step] + other[step]

    combine(2)
    slab_copies[2].start()
    for copy in proj_copies:
        copy.wait()

    def gathered(atom):
        parity = atom % 2
        found = jnp.zeros((2, NFUNC), F32)
        for j in range(3):
            found = found + every[(atom // 2 + j) % N_GRID, pl.ds(2 * (4 - 2 * j) + 2 * parity, 2), :]
        return found

    for m in range(NEAR):
        mine[pl.ds(2 * m, 2), :] = gathered((2 * me - 4 + m + N_ATOMS) % N_ATOMS)
    for s in range(OWN):
        atom = slots[me * OWN + s]
        found = gathered(jnp.maximum(atom, 0))
        mine[pl.ds(12 + 2 * s, 2), :] = jnp.where(atom >= 0, found, 0.0)
    mine[pl.ds(20, 4), :] = jnp.full((4, NFUNC), weight[0], F32)
    share_copies = []
    for step in range(1, NBANDS):
        copy = pltpu.make_async_remote_copy(
            src_ref=mine,
            dst_ref=shared.at[band],
            send_sem=share_send.at[step],
            recv_sem=share_recv.at[step],
            device_id={"band": (band + step) % NBANDS},
        )
        copy.start()
        share_copies.append(copy)
    for step in (1, 3):
        combine(step)
        slab_copies[step].start()
    combine(0)
    shared[band] = mine[...]
    for copy in share_copies:
        copy.wait()
    for b in range(NBANDS):
        for m in range(NEAR):
            near[pl.ds(m * 16 + 2 * b, 2), :] = shared[b, pl.ds(2 * m, 2), :]
        level[pl.ds(2 * b, 2), :] = shared[b, pl.ds(20, 2), :]
    weights = level[...]
    parts = split(near[...])
    wide = jnp.concatenate([weights, weights], axis=1)

    def one_layer(k, carry):
        value = mm3(parts, (aug_h[k], aug_l[k])).reshape(NEAR, 16, GRID)
        boxes[k, pl.ds(0, NEAR), :] = jnp.sum(value * value * wide[None], axis=1)
        return carry

    lax.fori_loop(0, BOX, one_layer, 0)
    for step in (1, 2, 3):
        slab_copies[step].wait()
    total[...] = (summed[0] + slabs[1]) + (slabs[2] + slabs[3])


def sums(slots, weight, proj, dens, aug_h, aug_l):
    quarter = (PLANES, 32, GRID)
    dma = pltpu.SemaphoreType.DMA
    return pl.pallas_call(
        sum_kernel,
        out_shape=(
            jax.ShapeDtypeStruct(quarter, F32),
            jax.ShapeDtypeStruct((NBANDS, 24, NFUNC), F32),
            jax.ShapeDtypeStruct((BOX, 8, GRID), F32),
        ),
        in_specs=[SM, SM, VM, ANY, VM, VM],
        out_specs=(VM, VM, VM),
        scratch_shapes=[
            pltpu.VMEM((N_GRID, 16, NFUNC), F32),
            pltpu.VMEM((24, NFUNC), F32),
            pltpu.VMEM((NEAR * 16, NFUNC), F32),
            pltpu.VMEM((16, NFUNC), F32),
            pltpu.VMEM((4,) + quarter, F32),
            pltpu.VMEM((4,) + quarter, F32),
            pltpu.VMEM((4,) + quarter, F32),
            pltpu.VMEM((4,) + quarter, F32),
            dma((4,)), dma((4,)), dma((4,)), dma((4,)), dma((4,)),
            dma((N_GRID,)), dma((N_GRID,)), dma((NBANDS,)), dma((NBANDS,)),
        ],
        compiler_params=pltpu.CompilerParams(collective_id=1, has_side_effects=True),
        name="sums",
    )(slots, weight, proj, dens, aug_h, aug_l)


def final_kernel(offsets, shared, total, boxes, dens, totals):
    me = lax.axis_index("grid")
    band = lax.axis_index("band")
    weights = jnp.concatenate([shared[b, pl.ds(20, 2), :] for b in range(NBANDS)], axis=0)
    for s in range(OWN):
        own = jnp.concatenate([shared[b, pl.ds(12 + 2 * s, 2), :] for b in range(NBANDS)], axis=0)
        totals[s] = lax.dot_general(
            own * weights,
            own,
            (((0,), (0,)), ((), ())),
            precision=lax.Precision.HIGHEST,
            preferred_element_type=F32,
        )
    dens[...] = total[...]
    row = lax.broadcasted_iota(jnp.int32, (32, GRID), 0)
    cell = lax.broadcasted_iota(jnp.int32, (32, GRID), 1) // BOX
    for m in range(NEAR):
        atom = (2 * me - 4 + m + N_ATOMS) % N_ATOMS
        x0, y0, z0 = offsets[0, atom], offsets[1, atom], offsets[2, atom]
        shift = (band * 32 - x0 + GRID) % GRID

        @pl.when((shift < BOX) | (shift > GRID - 32))
        def _():
            keep = cell == (row + shift) % GRID
            planes = []
            for plane in range(PLANES):
                k = (me * PLANES + plane - z0 + GRID) % GRID
                line = boxes[jnp.minimum(k, BOX - 1), pl.ds(m, 1), :]
                line = jnp.where(k < BOX, line, 0.0)
                planes.append(jnp.where(keep, line, 0.0))
            high, low = split(jnp.concatenate(planes, axis=0))
            pick = window_pick(y0)
            spot = mm(high, pick, NT) + mm(low, pick, NT)
            dens[...] += spot.reshape(PLANES, 32, GRID)


def final(offsets, shared, total, boxes):
    return pl.pallas_call(
        final_kernel,
        out_shape=(
            jax.ShapeDtypeStruct((PLANES, 32, GRID), F32),
            jax.ShapeDtypeStruct((OWN, NFUNC, NFUNC), F32),
        ),
        in_specs=[SM, VM, VM, VM],
        out_specs=(VM, VM),
        name="final",
    )(offsets, shared, total, boxes)


def on_device(coeffs, stick_ids, band_weights, aug_functions, atom_offsets, intersection_list, atom_slots):
    along_z, along_y, along_x = (halves(table) for table in tables())
    offsets = atom_offsets.T
    sticks = z_transform(coeffs.reshape(2, CAP, KG), *along_z)
    grid, aug_h, aug_l = exchange(stick_ids.reshape(N_GRID, 1, CAP), sticks, aug_functions)
    dens, proj = waves(offsets, band_weights, grid, *along_y, *along_x, aug_h, aug_l)
    total, shared, boxes = sums(atom_slots, band_weights, proj, dens, aug_h, aug_l)
    return final(offsets, shared, total, boxes)


def solution(mesh):
    placed = (P(None, "band", "grid", None), P(), P("band"), P(), P(), P("grid", None), P())
    return jax.shard_map(
        on_device,
        mesh=mesh,
        in_specs=placed,
        out_specs=(P("grid", "band", None), P("grid", None, None)),
        check_vma=False,
    )
```

```python
import functools

import jax
import jax.numpy as jnp
import numpy as np
from jax import lax
from jax.experimental import pallas as pl
from jax.experimental.pallas import tpu as pltpu
from jax.sharding import PartitionSpec as P

GRID = 256
KG = 128
PLANES = 8
BOX = 16
NFUNC = 128
NBANDS = 8
N_GRID = 32
N_ATOMS = 64
OWN = 4
CAP = 688
NEAR = 6
HIGH = 64
FULL = CAP // 128
REST = CAP % 128
TILES = 2 * FULL + 1
WIDE = FULL * 128 + 128
BF = jnp.bfloat16
F32 = jnp.float32
VM = pl.BlockSpec(memory_space=pltpu.VMEM)
SM = pl.BlockSpec(memory_space=pltpu.SMEM)
ANY = pl.BlockSpec(memory_space=pl.ANY)
NT = (((1,), (1,)), ((), ()))
NN = (((1,), (0,)), ((), ()))


def tables():
    frequency = np.arange(KG) - KG // 2
    angles = 2.0 * np.pi * ((frequency[:, None] * np.arange(GRID)[None, :]) % GRID) / GRID
    cosine = np.cos(angles) * KG ** -0.5
    sine = np.sin(angles) * KG ** -0.5
    to_real = np.concatenate([cosine, -sine], axis=0)
    to_imag = np.concatenate([sine, cosine], axis=0)
    along_z = np.stack([to_real.T, to_imag.T]).reshape(2, N_GRID, PLANES, 2 * KG)
    along_z = along_z.transpose(1, 0, 2, 3).reshape(2 * GRID, 2 * KG)
    along_y = np.concatenate([to_real, to_imag], axis=1)
    order = np.concatenate([np.arange(0, KG, 2), np.arange(1, KG, 2)])
    order = np.concatenate([order, order + KG])
    along_x = np.concatenate([to_real.T, to_imag.T], axis=0)[:, order]
    return along_z, along_y, along_x


def halves(table):
    high = table.astype(np.float32).astype(BF)
    low = (table - high.astype(np.float64)).astype(np.float32).astype(BF)
    return high, low


def split(value):
    high = value.astype(BF)
    return high, (value - high.astype(F32)).astype(BF)


def mm(left, right, dims=NN):
    return lax.dot_general(left, right, dims, preferred_element_type=F32)


def mm3(left, right, dims=NN):
    return mm(left[0], right[0], dims) + mm(left[1], right[0], dims) + mm(left[0], right[1], dims)


def exchange_kernel(
    coeffs, table_h, table_l, ids, aug, grid, aug_h, aug_l,
    sticks, land, names, held, part_h, part_l, aug_sem, send_sem, recv_sem,
):
    me = lax.axis_index("grid")
    z, y = me // 4, me % 4
    barrier = pltpu.get_barrier_semaphore()

    def offset(step):
        ring, turn = (step + 4) // 8, (step + 4) % 8
        edge = 1 - ((ring % 4) + 3) // 4
        dz = (ring * (1 - 2 * ((1 - edge) * (turn % 2))) + 8) % 8
        return dz, edge * (turn % 4) + (1 - edge) * (turn // 2)

    def target_at(step):
        dz, dy = offset(step)
        return ((z + dz) % 8) * 4 + (y + dy) % 4

    def copy_at(step):
        return pltpu.make_async_remote_copy(
            src_ref=sticks.at[step],
            dst_ref=land.at[step],
            send_sem=send_sem.at[step],
            recv_sem=recv_sem.at[step],
            device_id={"grid": target_at(step)},
        )

    for step in range(1, N_GRID):
        pl.semaphore_signal(barrier, inc=1, device_id={"grid": target_at(step)})
    fetch = pltpu.make_async_copy(aug, held, aug_sem)
    fetch.start()
    high, low = split(jnp.concatenate([coeffs[0], coeffs[1]], axis=1))
    part_h[...] = high
    part_l[...] = low

    def z_chunk(chunk):
        rows = [pl.ds(pl.multiple_of(target_at(chunk * 8 + j) * 16, 16), 16) for j in range(8)]
        left = (
            jnp.concatenate([table_h[r, :] for r in rows], axis=0),
            jnp.concatenate([table_l[r, :] for r in rows], axis=0),
        )
        got = mm3(left, (part_h[...], part_l[...]), NT).reshape(8, 16, CAP)
        where = pl.ds(chunk * 8, 8)
        for tile in range(FULL):
            lanes = slice(tile * 128, tile * 128 + 128)
            sticks[where, 2 * tile] = got[:, :8, lanes]
            sticks[where, 2 * tile + 1] = got[:, 8:, lanes]
        rest = got[:, :, FULL * 128 :]
        blank = jnp.zeros((8, 8, 128 - 2 * REST), F32)
        sticks[where, 2 * FULL] = jnp.concatenate([rest[:, :8], rest[:, 8:], blank], axis=2)

    z_chunk(0)
    z_chunk(1)
    pl.semaphore_wait(barrier, N_GRID - 1)
    for chunk in range(4):
        for step in range(max(1, chunk * 8), chunk * 8 + 8):
            copy_at(step).start()
        if chunk < 2:
            z_chunk(chunk + 2)
        elif chunk == 2:
            land[0] = sticks[0]
            names[...] = jnp.full_like(names, -1)
            for source in range(N_GRID):
                first, shift = source * CAP // 128, source * CAP % 128
                count = (shift + CAP + 127) // 128
                line = jnp.concatenate([ids[pl.ds(first + j, 1), :] for j in range(count)], axis=1)
                names[source, :, pl.ds(0, CAP)] = line[:, shift : shift + CAP]
    grid[...] = jnp.zeros_like(grid)
    fetch.wait()
    for k in range(BOX):
        high, low = split(held[:, k, :])
        aug_h[k] = high
        aug_l[k] = low

    row = lax.broadcasted_iota(jnp.int32, (HIGH, WIDE), 0)
    column = lax.broadcasted_iota(jnp.int32, (GRID, WIDE), 0)

    def one_pair(pair, carry):
        lefts, rights = [], []
        for step in (2 * pair, 2 * pair + 1):
            @pl.when(step > 0)
            def _():
                copy_at(step).wait()

        for step in (2 * pair, 2 * pair + 1):
            dz, dy = offset(step)
            name = names[((z - dz + 8) % 8) * 4 + (y - dy + 4) % 4]
            in_row = (row == (name >> 8)).astype(F32).astype(BF)
            in_column = (column == (name & (GRID - 1))).astype(F32).astype(BF)
            tiles = land[step]
            last = tiles[2 * FULL]
            top = [tiles[2 * tile] for tile in range(FULL)] + [last]
            bottom = [tiles[2 * tile + 1] for tile in range(FULL)] + [pltpu.roll(last, 128 - REST, 1)]
            value = jnp.concatenate([jnp.concatenate(top, axis=1), jnp.concatenate(bottom, axis=1)], axis=0)
            for half in split(value):
                lefts.append((in_row[None] * half[:, None, :]).reshape(16 * HIGH, WIDE))
                rights.append(in_column)
        got = mm(jnp.concatenate(lefts, axis=1), jnp.concatenate(rights, axis=1), NT)
        grid[...] += got.reshape(16, HIGH, GRID)
        return carry

    lax.fori_loop(0, N_GRID // 2, one_pair, 0)


def exchange(coeffs, high, low, ids, aug):
    return pl.pallas_call(
        exchange_kernel,
        out_shape=(
            jax.ShapeDtypeStruct((16, HIGH, GRID), F32),
            jax.ShapeDtypeStruct((BOX, NFUNC, GRID), BF),
            jax.ShapeDtypeStruct((BOX, NFUNC, GRID), BF),
        ),
        in_specs=[VM, VM, VM, VM, ANY],
        out_specs=(VM, VM, VM),
        scratch_shapes=[
            pltpu.VMEM((N_GRID, TILES, 8, 128), F32),
            pltpu.VMEM((N_GRID, TILES, 8, 128), F32),
            pltpu.VMEM((N_GRID, 1, WIDE), jnp.int32),
            pltpu.VMEM((NFUNC, BOX, GRID), F32),
            pltpu.VMEM((CAP, 2 * KG), BF),
            pltpu.VMEM((CAP, 2 * KG), BF),
            pltpu.SemaphoreType.DMA,
            pltpu.SemaphoreType.DMA((N_GRID,)),
            pltpu.SemaphoreType.DMA((N_GRID,)),
        ],
        compiler_params=pltpu.CompilerParams(collective_id=0, has_side_effects=True),
        name="stick_exchange",
    )(coeffs, high, low, ids, aug)


def window_pick(y0):
    cell = lax.broadcasted_iota(jnp.int32, (GRID, GRID), 1)
    place = lax.broadcasted_iota(jnp.int32, (GRID, GRID), 0)
    return (place == (y0 + cell % BOX) % GRID).astype(F32).astype(BF)


def wave_kernel(offsets, weight, grid, yh, yl, xh, xl, aug_h, aug_l, dens, proj, spec, wave, rows):
    me = lax.axis_index("grid")
    for parity in range(2):
        lanes = slice(parity * KG, parity * KG + KG)
        both = jnp.concatenate([grid[:8, :, lanes], grid[8:, :, lanes]], axis=2).reshape(8 * HIGH, GRID)
        got = mm3(split(both), (yh[...], yl[...])).reshape(8, HIGH, 2 * GRID)
        spec[:, pl.ds(parity * HIGH, HIGH), :] = got[:, :, :GRID]
        spec[:, pl.ds(parity * HIGH + KG, HIGH), :] = got[:, :, GRID:]

    scale = weight[0]

    def x_step(plane, carry):
        got = mm3((xh[...], xl[...]), split(spec[plane]))
        real, imag = got[:GRID], got[GRID:]
        wave[plane, 0, pl.ds(0, GRID), :] = real
        wave[plane, 1, pl.ds(0, GRID), :] = imag
        wave[plane, 0, pl.ds(GRID, 24), :] = real[:24]
        wave[plane, 1, pl.ds(GRID, 24), :] = imag[:24]
        local = (scale * (real * real + imag * imag)).reshape(4, 2, 32, GRID)
        dens[0, :, plane] = local[:, 0]
        dens[1, :, plane] = local[:, 1]
        return carry

    lax.fori_loop(0, PLANES, x_step, 0)

    rows[...] = jnp.zeros_like(rows)
    cell = lax.broadcasted_iota(jnp.int32, (24, GRID), 1) // BOX
    row = lax.broadcasted_iota(jnp.int32, (24, GRID), 0)

    def one_atom(m, carry):
        atom = (2 * me - 4 + m + N_ATOMS) % N_ATOMS
        x0, y0, z0 = offsets[0, atom], offsets[1, atom], offsets[2, atom]
        low_x = pl.multiple_of((x0 // 8) * 8, 8)
        window = wave[:, :, pl.ds(low_x, 24), :].reshape(16 * 24, GRID)
        high, low = split(window)
        pick = window_pick(y0)
        picked = (mm(high, pick) + mm(low, pick)).reshape(16, 24, GRID)
        keep = cell == row - (x0 - low_x)
        flat = jnp.sum(jnp.where(keep[None], picked, 0.0), axis=1)
        flat = flat.reshape(8, 2, GRID)
        for plane in range(PLANES):
            k = (me * PLANES + plane - z0 + GRID) % GRID

            @pl.when(k < BOX)
            def _():
                rows[k, pl.ds(2 * m, 2), :] = flat[plane]

        return carry

    for m in range(NEAR):
        one_atom(m, 0)

    def contract(k, total):
        return total + mm3(split(rows[k]), (aug_h[k], aug_l[k]), NT)

    proj[...] = lax.fori_loop(0, BOX, contract, jnp.zeros((16, NFUNC), F32))


def waves(offsets, weight, grid, yh, yl, xh, xl, aug_h, aug_l):
    return pl.pallas_call(
        wave_kernel,
        out_shape=(
            jax.ShapeDtypeStruct((2, 4, PLANES, 32, GRID), F32),
            jax.ShapeDtypeStruct((16, NFUNC), F32),
        ),
        in_specs=[SM, SM] + [VM] * 7,
        out_specs=(VM, VM),
        scratch_shapes=[
            pltpu.VMEM((PLANES, GRID, GRID), F32),
            pltpu.VMEM((PLANES, 2, GRID + 24, GRID), F32),
            pltpu.VMEM((BOX, 16, GRID), F32),
        ],
        name="waves",
    )(offsets, weight, grid, yh, yl, xh, xl, aug_h, aug_l)


def sum_kernel(
    slots, weight, proj, dens, aug_h, aug_l, total, shared, boxes,
    every, mine, near, level, half, other, summed, slabs,
    half_sem, pair_send, pair_recv, slab_send, slab_recv, proj_send, proj_recv, share_send, share_recv,
):
    me = lax.axis_index("grid")
    band = lax.axis_index("band")
    chip, core = band // 2, band % 2
    partner = chip * 2 + 1 - core
    barrier = pltpu.get_barrier_semaphore()
    for step in range(1, N_GRID):
        pl.semaphore_signal(barrier, inc=1, device_id={"grid": (me + step) % N_GRID})
    for step in range(1, NBANDS):
        pl.semaphore_signal(barrier, inc=1, device_id={"band": (band + step) % NBANDS})
    fetches = []
    for step in range(4):
        place = (chip + step) % 4
        fetches.append(pltpu.make_async_copy(dens.at[core, place], half.at[step], half_sem.at[step]))
        fetches[-1].start()
    pl.semaphore_wait(barrier, N_GRID + NBANDS - 2)

    pairs, slab_copies = [], []
    for step in range(4):
        place = (chip + step) % 4
        pairs.append(
            pltpu.make_async_remote_copy(
                src_ref=dens.at[1 - core, place],
                dst_ref=other.at[step],
                send_sem=pair_send.at[step],
                recv_sem=pair_recv.at[step],
                device_id={"band": partner},
            )
        )
        slab_copies.append(
            None
            if step == 0
            else pltpu.make_async_remote_copy(
                src_ref=summed.at[step],
                dst_ref=slabs.at[step],
                send_sem=slab_send.at[step],
                recv_sem=slab_recv.at[step],
                device_id={"band": place * 2 + core},
            )
        )
    pairs[2].start()
    proj_copies = []
    for step in range(1, N_GRID):
        copy = pltpu.make_async_remote_copy(
            src_ref=proj,
            dst_ref=every.at[me],
            send_sem=proj_send.at[step],
            recv_sem=proj_recv.at[step],
            device_id={"grid": (me + step) % N_GRID},
        )
        copy.start()
        proj_copies.append(copy)
    for step in (1, 3, 0):
        pairs[step].start()
    every[me] = proj[...]

    def combine(step):
        fetches[step].wait()
        pairs[step].wait()
        summed[step] = half[step] + other[step]

    combine(2)
    slab_copies[2].start()
    for copy in proj_copies:
        copy.wait()

    def gathered(atom):
        parity = atom % 2
        found = jnp.zeros((2, NFUNC), F32)
        for j in range(3):
            found = found + every[(atom // 2 + j) % N_GRID, pl.ds(2 * (4 - 2 * j) + 2 * parity, 2), :]
        return found

    for m in range(NEAR):
        mine[pl.ds(2 * m, 2), :] = gathered((2 * me - 4 + m + N_ATOMS) % N_ATOMS)
    for s in range(OWN):
        atom = slots[me * OWN + s]
        found = gathered(jnp.maximum(atom, 0))
        mine[pl.ds(12 + 2 * s, 2), :] = jnp.where(atom >= 0, found, 0.0)
    mine[pl.ds(20, 4), :] = jnp.full((4, NFUNC), weight[0], F32)
    share_copies = []
    for step in range(1, NBANDS):
        copy = pltpu.make_async_remote_copy(
            src_ref=mine,
            dst_ref=shared.at[band],
            send_sem=share_send.at[step],
            recv_sem=share_recv.at[step],
            device_id={"band": (band + step) % NBANDS},
        )
        copy.start()
        share_copies.append(copy)
    for step in (1, 3):
        combine(step)
        slab_copies[step].start()
    combine(0)
    shared[band] = mine[...]
    for copy in share_copies:
        copy.wait()
    for b in range(NBANDS):
        for m in range(NEAR):
            near[pl.ds(m * 16 + 2 * b, 2), :] = shared[b, pl.ds(2 * m, 2), :]
        level[pl.ds(2 * b, 2), :] = shared[b, pl.ds(20, 2), :]
    weights = level[...]
    parts = split(near[...])
    wide = jnp.concatenate([weights, weights], axis=1)

    def one_layer(k, carry):
        value = mm3(parts, (aug_h[k], aug_l[k])).reshape(NEAR, 16, GRID)
        boxes[k, pl.ds(0, NEAR), :] = jnp.sum(value * value * wide[None], axis=1)
        return carry

    lax.fori_loop(0, BOX, one_layer, 0)
    for step in (1, 2, 3):
        slab_copies[step].wait()
    total[...] = (summed[0] + slabs[1]) + (slabs[2] + slabs[3])


def sums(slots, weight, proj, dens, aug_h, aug_l):
    quarter = (PLANES, 32, GRID)
    dma = pltpu.SemaphoreType.DMA
    return pl.pallas_call(
        sum_kernel,
        out_shape=(
            jax.ShapeDtypeStruct(quarter, F32),
            jax.ShapeDtypeStruct((NBANDS, 24, NFUNC), F32),
            jax.ShapeDtypeStruct((BOX, 8, GRID), F32),
        ),
        in_specs=[SM, SM, VM, ANY, VM, VM],
        out_specs=(VM, VM, VM),
        scratch_shapes=[
            pltpu.VMEM((N_GRID, 16, NFUNC), F32),
            pltpu.VMEM((24, NFUNC), F32),
            pltpu.VMEM((NEAR * 16, NFUNC), F32),
            pltpu.VMEM((16, NFUNC), F32),
            pltpu.VMEM((4,) + quarter, F32),
            pltpu.VMEM((4,) + quarter, F32),
            pltpu.VMEM((4,) + quarter, F32),
            pltpu.VMEM((4,) + quarter, F32),
            dma((4,)), dma((4,)), dma((4,)), dma((4,)), dma((4,)),
            dma((N_GRID,)), dma((N_GRID,)), dma((NBANDS,)), dma((NBANDS,)),
        ],
        compiler_params=pltpu.CompilerParams(collective_id=1, has_side_effects=True),
        name="sums",
    )(slots, weight, proj, dens, aug_h, aug_l)


def final_kernel(offsets, shared, total, boxes, dens, totals):
    me = lax.axis_index("grid")
    band = lax.axis_index("band")
    weights = jnp.concatenate([shared[b, pl.ds(20, 2), :] for b in range(NBANDS)], axis=0)
    for s in range(OWN):
        own = jnp.concatenate([shared[b, pl.ds(12 + 2 * s, 2), :] for b in range(NBANDS)], axis=0)
        totals[s] = lax.dot_general(
            own * weights,
            own,
            (((0,), (0,)), ((), ())),
            precision=lax.Precision.HIGHEST,
            preferred_element_type=F32,
        )
    dens[...] = total[...]
    row = lax.broadcasted_iota(jnp.int32, (32, GRID), 0)
    cell = lax.broadcasted_iota(jnp.int32, (32, GRID), 1) // BOX
    for m in range(NEAR):
        atom = (2 * me - 4 + m + N_ATOMS) % N_ATOMS
        x0, y0, z0 = offsets[0, atom], offsets[1, atom], offsets[2, atom]
        shift = (band * 32 - x0 + GRID) % GRID

        @pl.when((shift < BOX) | (shift > GRID - 32))
        def _():
            keep = cell == (row + shift) % GRID
            planes = []
            for plane in range(PLANES):
                k = (me * PLANES + plane - z0 + GRID) % GRID
                line = boxes[jnp.minimum(k, BOX - 1), pl.ds(m, 1), :]
                line = jnp.where(k < BOX, line, 0.0)
                planes.append(jnp.where(keep, line, 0.0))
            high, low = split(jnp.concatenate(planes, axis=0))
            pick = window_pick(y0)
            spot = mm(high, pick, NT) + mm(low, pick, NT)
            dens[...] += spot.reshape(PLANES, 32, GRID)


def final(offsets, shared, total, boxes):
    return pl.pallas_call(
        final_kernel,
        out_shape=(
            jax.ShapeDtypeStruct((PLANES, 32, GRID), F32),
            jax.ShapeDtypeStruct((OWN, NFUNC, NFUNC), F32),
        ),
        in_specs=[SM, VM, VM, VM],
        out_specs=(VM, VM),
        name="final",
    )(offsets, shared, total, boxes)


def on_device(coeffs, stick_ids, band_weights, aug_functions, atom_offsets, intersection_list, atom_slots):
    along_z, along_y, along_x = (halves(table) for table in tables())
    offsets = atom_offsets.T
    ids = stick_ids.reshape(-1, 128)
    grid, aug_h, aug_l = exchange(coeffs.reshape(2, CAP, KG), *along_z, ids, aug_functions)
    dens, proj = waves(offsets, band_weights, grid, *along_y, *along_x, aug_h, aug_l)
    total, shared, boxes = sums(atom_slots, band_weights, proj, dens, aug_h, aug_l)
    return final(offsets, shared, total, boxes)


def solution(mesh):
    placed = (P(None, "band", "grid", None), P(), P("band"), P(), P(), P("grid", None), P())
    return jax.shard_map(
        on_device,
        mesh=mesh,
        in_specs=placed,
        out_specs=(P("grid", "band", None), P("grid", None, None)),
        check_vma=False,
    )
```
